1024 devices in a mesh: blk: 32 (over x, y_lo, core), group: 32 (over z, y_hi).
Axes of the slice: x: 4, y: 8 (y_hi: 2, y_lo: 4; y = y_hi * 4 + y_lo), z: 16, core: 2. Of those that a mesh axis runs over, the one named last changes fastest.
Arguments:
- row_factors: float32 [524288, 256], P(('blk', 'group')), may hold values from -0.45 to 0.45
- col_factors: float32 [524288, 256], P(('blk', 'group')), may hold values from -0.45 to 0.45
- tile_values: bfloat16 [5, 8192, 128, 128], P(None, ('blk', 'group')), may hold values from -4 to 4
- tile_coords: int32 [5, 8192, 2], P(None, ('blk', 'group')), may hold values from 0 to 3, as said below
- tile_counts: int32 [5, 1024], P(None, ('blk', 'group')), may hold values from 2 to 8, as said below
Outputs:
- rows_out: float32 [524288, 256], P(('blk', 'group'))
- cols_out: float32 [524288, 256], P(('blk', 'group'))
The draws below stay inside these ranges and needn't reach their ends.
Inputs may be any that keep to these rules, and one draw needn't show every extreme that they name: `tile_coords`: the 8 entries of one device and stratum name distinct tiles; the row tile is below 4, the column tile below 4. `tile_counts`: in every stratum some device lists 8 live tiles.
All inputs are finite; a program needn't handle non-finite values.
Results may differ from the reference program's by a relative error of at most 0.005.
Values sent between devices are 32-bit elements; how exact they have to be, the bound alone decides.
A program may use at most 32 MiB of HBM per device.

```python
import jax
import jax.numpy as jnp
from jax import lax

RANK = 256
TILE = 128
ROW_DEV = 512
COL_BLK = 512
MOST = 8
STRATA = 5
ROWS = 524288
COLS = 524288
N_BLK = 32
N_GROUP = 32
DEVICES = 1024


def factor_field(key, count):
    values = 0.15 * jax.random.normal(jax.random.fold_in(key, 3), (count, RANK), jnp.float32)
    return jnp.clip(values, -0.45, 0.45)


def draw_row_factors(key, part):
    return factor_field(jax.random.fold_in(key, 11), ROWS)


def draw_col_factors(key, part):
    return factor_field(jax.random.fold_in(key, 13), COLS)


def draw_tile_coords(key, part):
    col_tiles = COL_BLK // TILE
    places = ROW_DEV // TILE * col_tiles
    scores = jax.random.randint(key, (STRATA, DEVICES, places), 0, 1 << 20) * places + jnp.arange(places)
    ordering = jnp.argsort(scores, axis=-1, stable=True)[:, :, :MOST].astype(jnp.int32)
    stacked = jnp.stack([ordering // col_tiles, ordering % col_tiles], axis=-1)
    return stacked.reshape(STRATA, DEVICES * MOST, 2).astype(jnp.int32)


def draw_tile_counts(key, part):
    counts = jax.random.randint(key, (STRATA, DEVICES), max(1, MOST // 4), MOST + 1)
    busiest = (jnp.arange(STRATA) * 97 + 5) % DEVICES
    return counts.at[jnp.arange(STRATA), busiest].set(MOST).astype(jnp.int32)


def block_scale(rng, shape, shards, smallest, top_value):
    gain = 1.0
    for axis_at, blocks in shards:
        heights = jax.random.uniform(jax.random.fold_in(jax.random.fold_in(rng, 6), axis_at), (blocks,), jnp.float32, smallest / len(shards), top_value / len(shards))
        gain = gain * jnp.repeat(jnp.exp(heights), shape[axis_at] // blocks).reshape((-1,) + (1,) * (len(shape) - 1 - axis_at))
    return gain


def noise(rng, shape, deviation, most, split=(), dtype=jnp.bfloat16):
    array = deviation * jax.random.normal(rng, shape, jnp.float32)
    if split:
        array = array * block_scale(rng, shape, split, -0.22, 0.18)
    return jnp.clip(array, -most, most).astype(dtype)


def setup_inputs(seed: int = 0) -> dict:
    seeds = jax.random.split(jax.random.key(seed), 6)
    row_factors = draw_row_factors(jax.random.fold_in(seeds[5], 71), 0)
    col_factors = draw_col_factors(jax.random.fold_in(seeds[5], 71), 0)
    tile_values = noise(seeds[2], (STRATA, DEVICES * MOST, TILE, TILE), 1.0, 4.0, ((1, 1024),))
    tile_coords = draw_tile_coords(jax.random.fold_in(seeds[5], 71), 0)
    tile_counts = draw_tile_counts(jax.random.fold_in(seeds[5], 71), 0)
    return {"row_factors": row_factors, "col_factors": col_factors, "tile_values": tile_values, "tile_coords": tile_coords, "tile_counts": tile_counts}


LEARN_RATE = 0.03
DECAY_RATE = 0.1


def through_half(value):
    return lax.optimization_barrier(value.astype(jnp.bfloat16)).astype(jnp.float32)


def picker(positions, extent, live_mask):
    return (positions[:, None] == jnp.arange(extent)[None, :]).astype(jnp.float32) * live_mask[:, None]


def update(packed):
    row_block, col_block, values, tile_pos, tile_count = packed
    high = lax.Precision.HIGHEST
    row_tiles = ROW_DEV // TILE
    col_tiles = COL_BLK // TILE
    live_mask = (jnp.arange(MOST) < tile_count).astype(jnp.float32)
    row_pick = picker(tile_pos[:, 0], row_tiles, live_mask)
    col_pick = picker(tile_pos[:, 1], col_tiles, live_mask)
    row_half = through_half(row_block).reshape(row_tiles, TILE, RANK)
    col_half = through_half(col_block).reshape(col_tiles, TILE, RANK)
    row_sel = jnp.einsum('tk,kia->tia', row_pick, row_half, precision=high)
    col_sel = jnp.einsum('tk,kja->tja', col_pick, col_half, precision=high)
    estimate = jnp.einsum('tia,tja->tij', row_sel, col_sel, precision=high)
    residue = through_half(values.astype(jnp.float32) - estimate)
    row_terms = jnp.einsum('tij,tja->tia', residue, col_sel, precision=high)
    col_terms = jnp.einsum('tij,tia->tja', residue, row_sel, precision=high)
    grad_rows = jnp.einsum('tk,tia->kia', row_pick, row_terms, precision=high).reshape(ROW_DEV, RANK)
    grad_cols = jnp.einsum('tk,tja->kja', col_pick, col_terms, precision=high).reshape(COL_BLK, RANK)
    new_rows = row_block + LEARN_RATE * (grad_rows - DECAY_RATE * row_block)
    new_cols = col_block + LEARN_RATE * (grad_cols - DECAY_RATE * col_block)
    return new_rows, new_cols


def reference(row_factors, col_factors, tile_values, tile_coords, tile_counts):
    row_blocks = row_factors.reshape(DEVICES, ROW_DEV, RANK)
    held = col_factors.reshape(DEVICES, COL_BLK, RANK)
    for stratum in range(STRATA):
        values = tile_values[stratum].reshape(DEVICES, MOST, TILE, TILE)
        tile_pos = tile_coords[stratum].reshape(DEVICES, MOST, 2)
        row_blocks, held = lax.map(update, (row_blocks, held, values, tile_pos, tile_counts[stratum]))
        if stratum + 1 < STRATA:
            grid = held.reshape(N_BLK, N_GROUP, COL_BLK, RANK)
            if stratum == 2:
                grid = jnp.roll(grid, 1, axis=1)
            else:
                grid = jnp.roll(grid, 1, axis=0)
            held = grid.reshape(DEVICES, COL_BLK, RANK)
    return row_blocks.reshape(ROWS, RANK), held.reshape(COLS, RANK)
```

```python
import functools

import jax
import jax.numpy as jnp
from jax import lax
from jax.experimental import pallas as pl
from jax.experimental.pallas import tpu as pltpu
from jax.sharding import PartitionSpec as P

STRATA = 5
TILE = 128
MOST = 8
PIECES = 4

LEARN_RATE = 0.03
DECAY_RATE = 0.1

MESH = pl.DeviceIdType.MESH


def shift_axis(stratum):
    return "group" if stratum == 2 else "blk"


def neighbour(axis, distance, size):
    return {axis: lax.rem(lax.axis_index(axis) + size + distance, size)}


def find_slots(counts, coords, slots, lives, stratum, row_tiles, col_tiles):
    places = []
    for k in range(MOST):
        place = coords[stratum, 0, k] * col_tiles + coords[stratum, 1, k]
        places.append(jnp.where(k < counts[stratum], place, -1))
    for place in range(row_tiles * col_tiles):
        slot = jnp.int32(0)
        live = jnp.int32(0)
        for k in range(MOST):
            hit = places[k] == place
            slot = jnp.where(hit, k, slot)
            live = jnp.where(hit, 1, live)
        slots[stratum, place] = slot
        lives[stratum, place] = live.astype(jnp.float32)


def kernel(
    sizes, counts, coords, rows_in, cols_in, tiles_in, rows_out, cols_out,
    u, a, gu, held, sent, slots, lives, load_sem, send_sem, recv_sem, *tiles,
):
    rows = rows_in.shape[0]
    cols = cols_in.shape[0]
    row_tiles, col_tiles = rows // TILE, cols // TILE
    piece = cols // PIECES

    loads = [
        pltpu.make_async_copy(rows_in, u, load_sem.at[0]),
        pltpu.make_async_copy(cols_in, held.at[0], load_sem.at[1]),
    ]
    for stratum in range(STRATA):
        loads.append(pltpu.make_async_copy(tiles_in.at[stratum], tiles[stratum], load_sem.at[2 + stratum]))
    for load in loads:
        load.start()

    barrier = pltpu.get_barrier_semaphore()
    for axis in ("blk", "group"):
        pl.semaphore_signal(barrier, inc=1, device_id=neighbour(axis, -1, sizes[axis]), device_id_type=MESH)

    for stratum in range(STRATA):
        find_slots(counts, coords, slots, lives, stratum, row_tiles, col_tiles)

    copies = {}
    loads[0].wait()
    loads[1].wait()
    a[...] = u[...].astype(jnp.bfloat16)
    for stratum in range(STRATA):
        loads[2 + stratum].wait()
        last = stratum + 1 == STRATA
        for j in range(PIECES):
            span = pl.ds(j * piece, piece)
            if stratum:
                copies[stratum - 1, j].wait_recv()
            block = held[stratum, span, :]
            half = block.astype(jnp.bfloat16)
            estimate = lax.dot_general(
                a[...], half, (((1,), (1,)), ((), ())), preferred_element_type=jnp.float32
            )
            residues = []
            for i in range(row_tiles):
                place = i * col_tiles + j * piece // TILE
                values = tiles[stratum][slots[stratum, place]].astype(jnp.float32)
                error = values - estimate[i * TILE : (i + 1) * TILE, :]
                residues.append((error * lives[stratum, place]).astype(jnp.bfloat16))
            residue = jnp.concatenate(residues, axis=0)
            grad_cols = lax.dot_general(
                residue, a[...], (((0,), (0,)), ((), ())), preferred_element_type=jnp.float32
            )
            new_cols = block + LEARN_RATE * (grad_cols - DECAY_RATE * block)
            if last:
                cols_out[span, :] = new_cols
            else:
                sent[stratum, span, :] = new_cols
                if stratum == 0 and j == 0:
                    pl.semaphore_wait(barrier, 2)
                axis = shift_axis(stratum)
                copies[stratum, j] = pltpu.make_async_remote_copy(
                    src_ref=sent.at[stratum, span],
                    dst_ref=held.at[stratum + 1, span],
                    send_sem=send_sem.at[stratum, j],
                    recv_sem=recv_sem.at[stratum, j],
                    device_id=neighbour(axis, 1, sizes[axis]),
                    device_id_type=MESH,
                )
                copies[stratum, j].start()
            part = jnp.dot(residue, half, preferred_element_type=jnp.float32)
            if j == 0:
                gu[...] = part
            elif j + 1 < PIECES:
                gu[...] += part
            else:
                new_rows = u[...] + LEARN_RATE * ((gu[...] + part) - DECAY_RATE * u[...])
                if last:
                    rows_out[...] = new_rows
                else:
                    u[...] = new_rows
                    a[...] = new_rows.astype(jnp.bfloat16)
    for copy in copies.values():
        copy.wait_send()


def solution(mesh):
    sizes = dict(mesh.shape)

    def per_device(row_factors, col_factors, tile_values, tile_coords, tile_counts):
        rows, rank = row_factors.shape
        cols = col_factors.shape[0]
        out = pltpu.VMEM((rows, rank), jnp.float32)
        smem = pl.BlockSpec(memory_space=pltpu.SMEM)
        hbm = pl.BlockSpec(memory_space=pl.ANY)
        vmem = pl.BlockSpec(memory_space=pltpu.VMEM)
        places = (rows // TILE) * (cols // TILE)
        return pl.pallas_call(
            functools.partial(kernel, sizes),
            out_shape=(out, pltpu.VMEM((cols, rank), jnp.float32)),
            in_specs=[smem, smem, hbm, hbm, hbm],
            out_specs=(vmem, vmem),
            scratch_shapes=[
                pltpu.VMEM((rows, rank), jnp.float32),
                pltpu.VMEM((rows, rank), jnp.bfloat16),
                pltpu.VMEM((rows, rank), jnp.float32),
                pltpu.VMEM((STRATA, cols, rank), jnp.float32),
                pltpu.VMEM((STRATA - 1, cols, rank), jnp.float32),
                pltpu.SMEM((STRATA, places), jnp.int32),
                pltpu.SMEM((STRATA, places), jnp.float32),
                pltpu.SemaphoreType.DMA((2 + STRATA,)),
                pltpu.SemaphoreType.DMA((STRATA - 1, PIECES)),
                pltpu.SemaphoreType.DMA((STRATA - 1, PIECES)),
            ]
            + [pltpu.VMEM((MOST, TILE, TILE), jnp.bfloat16)] * STRATA,
            compiler_params=pltpu.CompilerParams(collective_id=0, has_side_effects=True),
            name="strata",
        )(
            tile_counts.reshape(STRATA),
            tile_coords.transpose(0, 2, 1),
            row_factors,
            col_factors,
            tile_values,
        )

    return jax.shard_map(
        per_device,
        mesh=mesh,
        in_specs=(
            P(("blk", "group"), None),
            P(("blk", "group"), None),
            P(None, ("blk", "group"), None, None),
            P(None, ("blk", "group"), None),
            P(None, ("blk", "group")),
        ),
        out_specs=(P(("blk", "group"), None), P(("blk", "group"), None)),
        check_vma=False,
    )
```

```python
import functools

import jax
import jax.numpy as jnp
from jax import lax
from jax.experimental import pallas as pl
from jax.experimental.pallas import tpu as pltpu
from jax.sharding import PartitionSpec as P

STRATA = 5
TILE = 128
MOST = 8
PIECES = 4
GATED = 2

LEARN_RATE = 0.03
DECAY_RATE = 0.1

MESH = pl.DeviceIdType.MESH


def shift_axis(stratum):
    return "group" if stratum == 2 else "blk"


def neighbour(axis, distance, size):
    return {axis: lax.rem(lax.axis_index(axis) + size + distance, size)}


def find_slots(counts, coords, slots, lives, stratum, row_tiles, col_tiles):
    places = []
    for k in range(MOST):
        place = coords[stratum, 0, k] * col_tiles + coords[stratum, 1, k]
        places.append(jnp.where(k < counts[stratum], place, -1))
    for place in range(row_tiles * col_tiles):
        slot = jnp.int32(0)
        live = jnp.int32(0)
        for k in range(MOST):
            hit = places[k] == place
            slot = jnp.where(hit, k, slot)
            live = jnp.where(hit, 1, live)
        slots[stratum, place] = slot
        lives[stratum, place] = live.astype(jnp.float32)


def kernel(
    sizes, counts, coords, rows_in, cols_in, tiles_in, rows_out, cols_out,
    u, a, gu, held, sent, slots, lives, load_sem, send_sem, recv_sem, gate, *tiles,
):
    rows = rows_in.shape[0]
    cols = cols_in.shape[0]
    row_tiles, col_tiles = rows // TILE, cols // TILE
    piece = cols // PIECES

    loads = [
        pltpu.make_async_copy(rows_in, u, load_sem.at[0]),
        pltpu.make_async_copy(cols_in, held.at[0], load_sem.at[1]),
    ]
    for stratum in range(STRATA):
        loads.append(pltpu.make_async_copy(tiles_in.at[stratum], tiles[stratum], load_sem.at[2 + stratum]))
    for load in loads:
        load.start()

    barrier = pltpu.get_barrier_semaphore()
    for axis, distance in (("blk", -1), ("blk", 1), ("group", -1)):
        pl.semaphore_signal(barrier, inc=1, device_id=neighbour(axis, distance, sizes[axis]), device_id_type=MESH)

    group = lax.axis_index("group")
    gated = (group > 0) & (group + 1 < sizes["group"])
    find_slots(counts, coords, slots, lives, 0, row_tiles, col_tiles)

    copies = {}
    loads[0].wait()
    loads[1].wait()
    a[...] = u[...].astype(jnp.bfloat16)
    for stratum in range(STRATA):
        if stratum:
            find_slots(counts, coords, slots, lives, stratum, row_tiles, col_tiles)
        loads[2 + stratum].wait()
        last = stratum + 1 == STRATA
        for j in range(PIECES):
            span = pl.ds(j * piece, piece)
            if stratum:
                copies[stratum - 1, j].wait_recv()
            block = held[stratum, span, :]
            half = block.astype(jnp.bfloat16)
            estimate = lax.dot_general(
                a[...], half, (((1,), (1,)), ((), ())), preferred_element_type=jnp.float32
            )
            residues = []
            for i in range(row_tiles):
                place = i * col_tiles + j * piece // TILE
                values = tiles[stratum][slots[stratum, place]].astype(jnp.float32)
                error = values - estimate[i * TILE : (i + 1) * TILE, :]
                residues.append((error * lives[stratum, place]).astype(jnp.bfloat16))
            residue = jnp.concatenate(residues, axis=0)
            grad_cols = lax.dot_general(
                residue, a[...], (((0,), (0,)), ((), ())), preferred_element_type=jnp.float32
            )
            new_cols = block + LEARN_RATE * (grad_cols - DECAY_RATE * block)
            if last:
                cols_out[span, :] = new_cols
            else:
                sent[stratum, span, :] = new_cols
                if stratum == 0 and j == 0:
                    pl.semaphore_wait(barrier, 3)
                axis = shift_axis(stratum)
                copies[stratum, j] = pltpu.make_async_remote_copy(
                    src_ref=sent.at[stratum, span],
                    dst_ref=held.at[stratum + 1, span],
                    send_sem=send_sem.at[stratum, j],
                    recv_sem=recv_sem.at[stratum, j],
                    device_id=neighbour(axis, 1, sizes[axis]),
                    device_id_type=MESH,
                )
                if stratum != GATED:
                    copies[stratum, j].start()
                else:
                    pl.when(jnp.logical_not(gated))(copies[stratum, j].start)
                if stratum == GATED and j + 1 == PIECES:
                    core = lax.rem(lax.axis_index("blk"), 2)
                    mate = {"blk": lax.axis_index("blk") + 1 - 2 * core}

                    @pl.when(gated)
                    def _():
                        pl.semaphore_signal(gate, inc=1, device_id=mate, device_id_type=MESH)
                        pl.semaphore_wait(gate, 1)
                        for at in range(PIECES):
                            copies[stratum, at].start()

            part = jnp.dot(residue, half, preferred_element_type=jnp.float32)
            if j == 0:
                gu[...] = part
            elif j + 1 < PIECES:
                gu[...] += part
            else:
                new_rows = u[...] + LEARN_RATE * ((gu[...] + part) - DECAY_RATE * u[...])
                if last:
                    rows_out[...] = new_rows
                else:
                    u[...] = new_rows
                    a[...] = new_rows.astype(jnp.bfloat16)
    for copy in copies.values():
        copy.wait_send()


def solution(mesh):
    sizes = dict(mesh.shape)

    def per_device(row_factors, col_factors, tile_values, tile_coords, tile_counts):
        rows, rank = row_factors.shape
        cols = col_factors.shape[0]
        out = pltpu.VMEM((rows, rank), jnp.float32)
        smem = pl.BlockSpec(memory_space=pltpu.SMEM)
        hbm = pl.BlockSpec(memory_space=pl.ANY)
        vmem = pl.BlockSpec(memory_space=pltpu.VMEM)
        places = (rows // TILE) * (cols // TILE)
        return pl.pallas_call(
            functools.partial(kernel, sizes),
            out_shape=(out, pltpu.VMEM((cols, rank), jnp.float32)),
            in_specs=[smem, smem, hbm, hbm, hbm],
            out_specs=(vmem, vmem),
            scratch_shapes=[
                pltpu.VMEM((rows, rank), jnp.float32),
                pltpu.VMEM((rows, rank), jnp.bfloat16),
                pltpu.VMEM((rows, rank), jnp.float32),
                pltpu.VMEM((STRATA, cols, rank), jnp.float32),
                pltpu.VMEM((STRATA - 1, cols, rank), jnp.float32),
                pltpu.SMEM((STRATA, places), jnp.int32),
                pltpu.SMEM((STRATA, places), jnp.float32),
                pltpu.SemaphoreType.DMA((2 + STRATA,)),
                pltpu.SemaphoreType.DMA((STRATA - 1, PIECES)),
                pltpu.SemaphoreType.DMA((STRATA - 1, PIECES)),
                pltpu.SemaphoreType.REGULAR,
            ]
            + [pltpu.VMEM((MOST, TILE, TILE), jnp.bfloat16)] * STRATA,
            compiler_params=pltpu.CompilerParams(collective_id=0, has_side_effects=True),
            name="strata",
        )(
            tile_counts.reshape(STRATA),
            tile_coords.transpose(0, 2, 1),
            row_factors,
            col_factors,
            tile_values,
        )

    return jax.shard_map(
        per_device,
        mesh=mesh,
        in_specs=(
            P(("blk", "group"), None),
            P(("blk", "group"), None),
            P(None, ("blk", "group"), None, None),
            P(None, ("blk", "group"), None),
            P(None, ("blk", "group")),
        ),
        out_specs=(P(("blk", "group"), None), P(("blk", "group"), None)),
        check_vma=False,
    )
```

```python
import functools

import jax
import jax.numpy as jnp
from jax import lax
from jax.experimental import pallas as pl
from jax.experimental.pallas import tpu as pltpu
from jax.sharding import PartitionSpec as P

STRATA = 5
TILE = 128
MOST = 8
PIECES = 4
GATED = 2

LEARN_RATE = 0.03
DECAY_RATE = 0.1

MESH = pl.DeviceIdType.MESH


def shift_axis(stratum):
    return "group" if stratum == 2 else "blk"


def neighbour(axis, distance, size):
    return {axis: lax.rem(lax.axis_index(axis) + size + distance, size)}


def find_slots(counts, coords, slots, lives, stratum, row_tiles, col_tiles):
    places = []
    for k in range(MOST):
        place = coords[stratum, 0, k] * col_tiles + coords[stratum, 1, k]
        places.append(jnp.where(k < counts[stratum], place, -1))
    for place in range(row_tiles * col_tiles):
        slot = jnp.int32(0)
        live = jnp.int32(0)
        for k in range(MOST):
            hit = places[k] == place
            slot = jnp.where(hit, k, slot)
            live = jnp.where(hit, 1, live)
        slots[stratum, place] = slot
        lives[stratum, place] = live.astype(jnp.float32)


def kernel(
    sizes, counts_in, coords_in, rows_in, cols_in, tiles_in, both_out,
    u, a, gu, held, sent, slots, lives, load_sem, send_sem, recv_sem, gate, counts, coords, table_sem, *tiles,
):
    rows = rows_in.shape[0]
    cols = cols_in.shape[0]
    rows_out, cols_out = both_out.at[pl.ds(0, rows)], both_out.at[pl.ds(rows, cols)]
    row_tiles, col_tiles = rows // TILE, cols // TILE
    piece = cols // PIECES

    tables = [
        pltpu.make_async_copy(counts_in, counts, table_sem.at[0]),
        pltpu.make_async_copy(coords_in, coords, table_sem.at[1]),
    ]
    for table in tables:
        table.start()
    loads = [
        pltpu.make_async_copy(rows_in, u, load_sem.at[0]),
        pltpu.make_async_copy(cols_in, held.at[0], load_sem.at[1]),
    ]
    for stratum in range(STRATA):
        loads.append(pltpu.make_async_copy(tiles_in.at[stratum], tiles[stratum], load_sem.at[2 + stratum]))
    for load in loads[:3]:
        load.start()

    barrier = pltpu.get_barrier_semaphore()
    for axis, distance in (("blk", -1), ("blk", 1), ("group", -1)):
        pl.semaphore_signal(barrier, inc=1, device_id=neighbour(axis, distance, sizes[axis]), device_id_type=MESH)

    group = lax.axis_index("group")
    gated = (group > 0) & (group + 1 < sizes["group"])
    for table in tables:
        table.wait()
    find_slots(counts, coords, slots, lives, 0, row_tiles, col_tiles)

    copies = {}
    loads[0].wait()
    loads[1].wait()
    loads[2].wait()
    for load in loads[3:]:
        load.start()
    a[...] = u[...].astype(jnp.bfloat16)
    for stratum in range(STRATA):
        if stratum:
            find_slots(counts, coords, slots, lives, stratum, row_tiles, col_tiles)
            loads[2 + stratum].wait()
        last = stratum + 1 == STRATA
        for j in range(PIECES):
            span = pl.ds(j * piece, piece)
            if stratum:
                copies[stratum - 1, j].wait_recv()
            block = held[stratum, span, :]
            half = block.astype(jnp.bfloat16)
            estimate = lax.dot_general(
                a[...], half, (((1,), (1,)), ((), ())), preferred_element_type=jnp.float32
            )
            residues = []
            for i in range(row_tiles):
                place = i * col_tiles + j * piece // TILE
                values = tiles[stratum][slots[stratum, place]].astype(jnp.float32)
                error = values - estimate[i * TILE : (i + 1) * TILE, :]
                residues.append((error * lives[stratum, place]).astype(jnp.bfloat16))
            residue = jnp.concatenate(residues, axis=0)
            grad_cols = lax.dot_general(
                residue, a[...], (((0,), (0,)), ((), ())), preferred_element_type=jnp.float32
            )
            new_cols = block + LEARN_RATE * (grad_cols - DECAY_RATE * block)
            if last:
                cols_out[span, :] = new_cols
            else:
                sent[stratum, span, :] = new_cols
                if stratum == 0 and j == 0:
                    pl.semaphore_wait(barrier, 3)
                axis = shift_axis(stratum)
                copies[stratum, j] = pltpu.make_async_remote_copy(
                    src_ref=sent.at[stratum, span],
                    dst_ref=held.at[stratum + 1, span],
                    send_sem=send_sem.at[stratum, j],
                    recv_sem=recv_sem.at[stratum, j],
                    device_id=neighbour(axis, 1, sizes[axis]),
                    device_id_type=MESH,
                )
                if stratum != GATED:
                    copies[stratum, j].start()
                else:
                    pl.when(jnp.logical_not(gated))(copies[stratum, j].start)
                if stratum == GATED and j + 1 == PIECES:
                    core = lax.rem(lax.axis_index("blk"), 2)
                    mate = {"blk": lax.axis_index("blk") + 1 - 2 * core}

                    @pl.when(gated)
                    def _():
                        pl.semaphore_signal(gate, inc=1, device_id=mate, device_id_type=MESH)
                        pl.semaphore_wait(gate, 1)
                        for at in range(PIECES):
                            copies[stratum, at].start()

            part = jnp.dot(residue, half, preferred_element_type=jnp.float32)
            if j == 0:
                gu[...] = part
            elif j + 1 < PIECES:
                gu[...] += part
            else:
                new_rows = u[...] + LEARN_RATE * ((gu[...] + part) - DECAY_RATE * u[...])
                if last:
                    rows_out[...] = new_rows
                else:
                    u[...] = new_rows
                    a[...] = new_rows.astype(jnp.bfloat16)
    for copy in copies.values():
        copy.wait_send()


def solution(mesh):
    sizes = dict(mesh.shape)

    def per_device(row_factors, col_factors, tile_values, tile_coords, tile_counts):
        rows, rank = row_factors.shape
        cols = col_factors.shape[0]
        hbm = pl.BlockSpec(memory_space=pl.ANY)
        vmem = pl.BlockSpec(memory_space=pltpu.VMEM)
        places = (rows // TILE) * (cols // TILE)
        both = pl.pallas_call(
            functools.partial(kernel, sizes),
            out_shape=pltpu.VMEM((rows + cols, rank), jnp.float32),
            in_specs=[hbm, hbm, hbm, hbm, hbm],
            out_specs=vmem,
            scratch_shapes=[
                pltpu.VMEM((rows, rank), jnp.float32),
                pltpu.VMEM((rows, rank), jnp.bfloat16),
                pltpu.VMEM((rows, rank), jnp.float32),
                pltpu.VMEM((STRATA, cols, rank), jnp.float32),
                pltpu.VMEM((STRATA - 1, cols, rank), jnp.float32),
                pltpu.SMEM((STRATA, places), jnp.int32),
                pltpu.SMEM((STRATA, places), jnp.float32),
                pltpu.SemaphoreType.DMA((2 + STRATA,)),
                pltpu.SemaphoreType.DMA((STRATA - 1, PIECES)),
                pltpu.SemaphoreType.DMA((STRATA - 1, PIECES)),
                pltpu.SemaphoreType.REGULAR,
                pltpu.SMEM((STRATA,), jnp.int32),
                pltpu.SMEM((STRATA, 2, MOST), jnp.int32),
                pltpu.SemaphoreType.DMA((2,)),
            ]
            + [pltpu.VMEM((MOST, TILE, TILE), jnp.bfloat16)] * STRATA,
            compiler_params=pltpu.CompilerParams(collective_id=0, has_side_effects=True),
            name="strata",
        )(
            tile_counts.reshape(STRATA),
            tile_coords.transpose(0, 2, 1),
            row_factors,
            col_factors,
            tile_values,
        )
        return both[:rows], both[rows:]

    return jax.shard_map(
        per_device,
        mesh=mesh,
        in_specs=(
            P(("blk", "group"), None),
            P(("blk", "group"), None),
            P(None, ("blk", "group"), None, None),
            P(None, ("blk", "group"), None),
            P(None, ("blk", "group")),
        ),
        out_specs=(P(("blk", "group"), None), P(("blk", "group"), None)),
        check_vma=False,
    )
```

```python
import functools

import jax
import jax.numpy as jnp
from jax import lax
from jax.experimental import pallas as pl
from jax.experimental.pallas import tpu as pltpu
from jax.sharding import PartitionSpec as P

STRATA = 5
TILE = 128
MOST = 8
PIECES = 4
GATED = 2

LEARN_RATE = 0.03
DECAY_RATE = 0.1

MESH = pl.DeviceIdType.MESH


def shift_axis(stratum):
    return "group" if stratum == 2 else "blk"


def neighbour(axis, distance, size):
    return {axis: lax.rem(lax.axis_index(axis) + size + distance, size)}


def find_slots(counts, coords, slots, lives, stratum, row_tiles, col_tiles):
    places = []
    for k in range(MOST):
        place = coords[stratum, 0, k] * col_tiles + coords[stratum, 1, k]
        places.append(jnp.where(k < counts[stratum], place, -1))
    for place in range(row_tiles * col_tiles):
        slot = jnp.int32(0)
        live = jnp.int32(0)
        for k in range(MOST):
            hit = places[k] == place
            slot = jnp.where(hit, k, slot)
            live = jnp.where(hit, 1, live)
        slots[stratum, place] = slot
        lives[stratum, place] = live.astype(jnp.float32)


def kernel(
    sizes, counts_in, coords_in, rows_in, cols_in, tiles_in, both_out,
    u, a, gu, held, sent, slots, lives, load_sem, send_sem, recv_sem, gate, counts, coords, table_sem, *tiles,
):
    rows = rows_in.shape[0]
    cols = cols_in.shape[0]
    rows_out, cols_out = both_out.at[pl.ds(0, rows)], both_out.at[pl.ds(rows, cols)]
    row_tiles, col_tiles = rows // TILE, cols // TILE
    piece = cols // PIECES

    tables = [
        pltpu.make_async_copy(counts_in, counts, table_sem.at[0]),
        pltpu.make_async_copy(coords_in, coords, table_sem.at[1]),
    ]
    for table in tables:
        table.start()
    loads = [
        pltpu.make_async_copy(rows_in, u, load_sem.at[0]),
        pltpu.make_async_copy(cols_in, held.at[0], load_sem.at[1]),
    ]
    for stratum in range(STRATA):
        loads.append(pltpu.make_async_copy(tiles_in.at[stratum], tiles[stratum], load_sem.at[2 + stratum]))
    for load in loads[:3]:
        load.start()

    barrier = pltpu.get_barrier_semaphore()
    for axis, distance in (("blk", -1), ("blk", 1), ("group", -1)):
        pl.semaphore_signal(barrier, inc=1, device_id=neighbour(axis, distance, sizes[axis]), device_id_type=MESH)

    group = lax.axis_index("group")
    gated = (group > 0) & (group + 1 < sizes["group"])
    for table in tables:
        table.wait()
    find_slots(counts, coords, slots, lives, 0, row_tiles, col_tiles)

    copies = {}
    loads[0].wait()
    loads[1].wait()
    loads[2].wait()
    for load in loads[3:]:
        load.start()
    a[...] = u[...].astype(jnp.bfloat16)
    for stratum in range(STRATA):
        if stratum == 1:
            find_slots(counts, coords, slots, lives, stratum, row_tiles, col_tiles)
        if stratum:
            loads[2 + stratum].wait()
        last = stratum + 1 == STRATA
        for j in range(PIECES):
            span = pl.ds(j * piece, piece)
            if stratum:
                if j + 1 == PIECES and not last:
                    find_slots(counts, coords, slots, lives, stratum + 1, row_tiles, col_tiles)
                copies[stratum - 1, j].wait_recv()
            block = held[stratum, span, :]
            half = block.astype(jnp.bfloat16)
            estimate = lax.dot_general(
                a[...], half, (((1,), (1,)), ((), ())), preferred_element_type=jnp.float32
            )
            residues = []
            for i in range(row_tiles):
                place = i * col_tiles + j * piece // TILE
                values = tiles[stratum][slots[stratum, place]].astype(jnp.float32)
                error = values - estimate[i * TILE : (i + 1) * TILE, :]
                residues.append((error * lives[stratum, place]).astype(jnp.bfloat16))
            residue = jnp.concatenate(residues, axis=0)
            grad_cols = lax.dot_general(
                residue, a[...], (((0,), (0,)), ((), ())), preferred_element_type=jnp.float32
            )
            new_cols = block + LEARN_RATE * (grad_cols - DECAY_RATE * block)
            if last:
                cols_out[span, :] = new_cols
            else:
                sent[stratum, span, :] = new_cols
                if stratum == 0 and j == 0:
                    pl.semaphore_wait(barrier, 3)
                axis = shift_axis(stratum)
                copies[stratum, j] = pltpu.make_async_remote_copy(
                    src_ref=sent.at[stratum, span],
                    dst_ref=held.at[stratum + 1, span],
                    send_sem=send_sem.at[stratum, j],
                    recv_sem=recv_sem.at[stratum, j],
                    device_id=neighbour(axis, 1, sizes[axis]),
                    device_id_type=MESH,
                )
                if stratum != GATED:
                    copies[stratum, j].start()
                else:
                    pl.when(jnp.logical_not(gated))(copies[stratum, j].start)
                if stratum == GATED and j + 1 == PIECES:
                    core = lax.rem(lax.axis_index("blk"), 2)
                    mate = {"blk": lax.axis_index("blk") + 1 - 2 * core}

                    @pl.when(gated)
                    def _():
                        pl.semaphore_signal(gate, inc=1, device_id=mate, device_id_type=MESH)
                        pl.semaphore_wait(gate, 1)
                        for at in range(PIECES):
                            copies[stratum, at].start()

            part = jnp.dot(residue, half, preferred_element_type=jnp.float32)
            if j == 0:
                gu[...] = part
            elif j + 1 < PIECES:
                gu[...] += part
            else:
                new_rows = u[...] + LEARN_RATE * ((gu[...] + part) - DECAY_RATE * u[...])
                if last:
                    rows_out[...] = new_rows
                else:
                    u[...] = new_rows
                    a[...] = new_rows.astype(jnp.bfloat16)
    for copy in copies.values():
        copy.wait_send()


def solution(mesh):
    sizes = dict(mesh.shape)

    def per_device(row_factors, col_factors, tile_values, tile_coords, tile_counts):
        rows, rank = row_factors.shape
        cols = col_factors.shape[0]
        hbm = pl.BlockSpec(memory_space=pl.ANY)
        vmem = pl.BlockSpec(memory_space=pltpu.VMEM)
        places = (rows // TILE) * (cols // TILE)
        both = pl.pallas_call(
            functools.partial(kernel, sizes),
            out_shape=pltpu.VMEM((rows + cols, rank), jnp.float32),
            in_specs=[hbm, hbm, hbm, hbm, hbm],
            out_specs=vmem,
            scratch_shapes=[
                pltpu.VMEM((rows, rank), jnp.float32),
                pltpu.VMEM((rows, rank), jnp.bfloat16),
                pltpu.VMEM((rows, rank), jnp.float32),
                pltpu.VMEM((STRATA, cols, rank), jnp.float32),
                pltpu.VMEM((STRATA - 1, cols, rank), jnp.float32),
                pltpu.SMEM((STRATA, places), jnp.int32),
                pltpu.SMEM((STRATA, places), jnp.float32),
                pltpu.SemaphoreType.DMA((2 + STRATA,)),
                pltpu.SemaphoreType.DMA((STRATA - 1, PIECES)),
                pltpu.SemaphoreType.DMA((STRATA - 1, PIECES)),
                pltpu.SemaphoreType.REGULAR,
                pltpu.SMEM((STRATA,), jnp.int32),
                pltpu.SMEM((STRATA, 2, MOST), jnp.int32),
                pltpu.SemaphoreType.DMA((2,)),
            ]
            + [pltpu.VMEM((MOST, TILE, TILE), jnp.bfloat16)] * STRATA,
            compiler_params=pltpu.CompilerParams(collective_id=0, has_side_effects=True),
            name="strata",
        )(
            tile_counts.reshape(STRATA),
            tile_coords.transpose(0, 2, 1),
            row_factors,
            col_factors,
            tile_values,
        )
        return both[:rows], both[rows:]

    return jax.shard_map(
        per_device,
        mesh=mesh,
        in_specs=(
            P(("blk", "group"), None),
            P(("blk", "group"), None),
            P(None, ("blk", "group"), None, None),
            P(None, ("blk", "group"), None),
            P(None, ("blk", "group")),
        ),
        out_specs=(P(("blk", "group"), None), P(("blk", "group"), None)),
        check_vma=False,
    )
```
